32 devices in a mesh: region: 16 (over z, y, x), tm: 2 (over core).
Axes of the slice: x: 2, y: 2, z: 4, core: 2. Of those that a mesh axis runs over, the one named last changes fastest.
Arguments:
- latents: bfloat16 [16, 256, 768], P('region', 'tm')
- output_grad: bfloat16 [16, 256, 768], P('region', 'tm'), may hold values from -6 to 6
- conv_kernel: float32 [4, 768], replicated, may hold values from -1 to 1
- w_query: bfloat16 [768, 768], replicated, may hold values from -0.21875 to 0.21875
- w_key: bfloat16 [768, 768], replicated, may hold values from -0.21875 to 0.21875
- w_value: bfloat16 [768, 768], replicated, may hold values from -0.21875 to 0.21875
- w_out: bfloat16 [768, 768], replicated, may hold values from -0.21875 to 0.21875
- live_counts: int32 [16, 2], P('region', 'tm'), may hold values from 1 to 128, as said below
Outputs:
- input_grad: bfloat16 [16, 256, 768], P('region', 'tm')
The draws below stay inside these ranges and needn't reach their ends.
Inputs may be any that keep to these rules, and one draw needn't show every extreme that they name: The first live_counts[r, c] of the 128 tokens of region r in span c are valid.
All inputs are finite; a program needn't handle non-finite values.
Results may differ from the reference program's by a relative error of at most 0.018.
The reference program's roundings to bfloat16 on the way (of `hidden`, `grad_proj`, `score_grad` and `query_grad`) count: a program that leaves them out, or rounds other values in their place, can miss the bound.
Values may be sent and summed in bfloat16 or wider, within the bound.
A program may use at most 128 MiB of HBM per device.

```python
import math
import jax
import jax.numpy as jnp
from jax import lax

D = 768
H = 12
HD = 64
KW = 4
TCH = 128
REGIONS = 16
TIME = 256
N_REGION = 16
N_TM = 2


def draw_latents(key, part):
    base = jax.random.normal(key, (REGIONS, TIME, D), jnp.float32)
    return base.astype(jnp.bfloat16)


def draw_live_counts(key, part):
    first = jax.random.randint(jax.random.fold_in(key, 11), (REGIONS, N_TM), 1, TCH + 1)
    second = jax.random.randint(jax.random.fold_in(key, 12), (REGIONS, N_TM), 1, TCH + 1)
    counts = jnp.minimum(first, second)
    counts = counts.at[0].set(TCH)
    return counts.astype(jnp.int32)


def steps_of(stream_key, dims, cuts, least, high):
    gain = 1.0
    for dim, shards_of in cuts:
        steps = jax.random.uniform(jax.random.fold_in(jax.random.fold_in(stream_key, 6), dim), (shards_of,), jnp.float32, least / len(cuts), high / len(cuts))
        gain = gain * jnp.repeat(jnp.exp(steps), dims[dim] // shards_of).reshape((-1,) + (1,) * (len(dims) - 1 - dim))
    return gain


def scatter_about(key, extent, spread, bound, pieces=(), kind=jnp.bfloat16):
    values = spread * jax.random.normal(key, extent, jnp.float32)
    if pieces:
        values = values * steps_of(key, extent, pieces, -0.22, 0.18)
    return jnp.clip(values, -bound, bound).astype(kind)


def setup_inputs(seed: int = 0) -> dict:
    splits = jax.random.split(jax.random.key(seed), 9)
    return {
        "latents": draw_latents(jax.random.fold_in(splits[8], 71), 0),
        "output_grad": scatter_about(splits[1], (REGIONS, TIME, D), 1.0, 6.0, ((0, 16), (1, 2))),
        "conv_kernel": jnp.clip(jax.random.uniform(splits[2], (KW, D), jnp.float32, -1.0, 1.0), -1.0, 1.0),
        "w_query": scatter_about(splits[3], (D, D), D ** -0.5, 0.21875),
        "w_key": scatter_about(splits[4], (D, D), D ** -0.5, 0.21875),
        "w_value": scatter_about(splits[5], (D, D), D ** -0.5, 0.21875),
        "w_out": scatter_about(splits[6], (D, D), D ** -0.5, 0.21875),
        "live_counts": draw_live_counts(jax.random.fold_in(splits[8], 71), 0),
    }


def rounded(values_in):
    return lax.optimization_barrier(values_in.astype(jnp.bfloat16)).astype(jnp.float32)

def causal_conv(signal, kernel):
    length = signal.shape[1]
    padded = jnp.pad(signal, ((0, 0), (KW - 1, 0), (0, 0)))
    result = jnp.zeros_like(signal)
    for offset in range(KW):
        result = result + kernel[offset] * padded[:, KW - 1 - offset:KW - 1 - offset + length, :]
    return result

def conv_transpose(grads, kernel):
    length = grads.shape[1]
    padded = jnp.pad(grads, ((0, 0), (0, KW - 1), (0, 0)))
    result = jnp.zeros_like(grads)
    for offset in range(KW):
        result = result + kernel[offset] * padded[:, offset:offset + length, :]
    return result

def head_grads(operands):
    query_rows, key_rows, value_rows, grad_rows, key_mask = operands
    inv_root = 1.0 / math.sqrt(HD)
    logits = jnp.where(key_mask[None, :], jnp.dot(query_rows, key_rows.T) * inv_root, -1e+30)
    top_logit = lax.optimization_barrier(jnp.max(logits, axis=1, keepdims=True))
    log_total = top_logit + jnp.log(lax.optimization_barrier(jnp.sum(jnp.exp(logits - top_logit), axis=1, keepdims=True)))
    attention = jnp.exp(logits - log_total)
    weight_grad = jnp.dot(grad_rows, value_rows.T)
    row_delta = lax.optimization_barrier(jnp.sum(attention * weight_grad, axis=1, keepdims=True))
    score_grad = rounded(attention * (weight_grad - row_delta))
    query_grad = jnp.dot(score_grad, key_rows) * inv_root
    groups = N_REGION
    per_group = query_rows.shape[0] // groups
    key_count = key_rows.shape[0]
    key_part = jnp.einsum('gqk,gqd->gkd', score_grad.reshape(groups, per_group, key_count), query_rows.reshape(groups, per_group, HD)) * inv_root
    value_part = jnp.einsum('gqk,gqd->gkd', rounded(attention).reshape(groups, per_group, key_count), grad_rows.reshape(groups, per_group, HD))
    key_sum = rounded(lax.optimization_barrier(jnp.sum(rounded(key_part), axis=0)))
    value_sum = rounded(lax.optimization_barrier(jnp.sum(rounded(value_part), axis=0)))
    return (query_grad, key_sum, value_sum)

def make_span_grads(w_key, w_value):

    def span_grads(operands):
        query_rows, key_rows, value_rows, grad_rows, key_mask = operands

        def heads_first(array_in):
            return array_in.astype(jnp.float32).reshape(-1, H, HD).transpose(1, 0, 2)
        head_masks = jnp.broadcast_to(key_mask, (H, key_mask.shape[0]))
        query_part, key_sum, value_sum = lax.map(head_grads, (heads_first(query_rows), heads_first(key_rows), heads_first(value_rows), heads_first(grad_rows), head_masks))

        def flat_rows(array_in):
            return array_in.transpose(1, 0, 2).reshape(-1, H * HD).astype(jnp.bfloat16)
        side_grad = jnp.dot(flat_rows(key_sum), w_key.T, preferred_element_type=jnp.float32)
        side_grad = side_grad + jnp.dot(flat_rows(value_sum), w_value.T, preferred_element_type=jnp.float32)
        return (query_part.transpose(1, 0, 2).reshape(-1, H * HD), side_grad)
    return span_grads

def reference(latents, output_grad, conv_kernel, w_query, w_key, w_value, w_out, live_counts):
    regions, total_time, model_width = latents.shape
    hidden = causal_conv(latents.astype(jnp.float32), conv_kernel).astype(jnp.bfloat16)
    flattened = hidden.reshape(-1, model_width)
    queries = jnp.dot(flattened, w_query, preferred_element_type=jnp.float32).astype(jnp.bfloat16)
    key_proj = jnp.dot(flattened, w_key, preferred_element_type=jnp.float32).astype(jnp.bfloat16)
    value_proj = jnp.dot(flattened, w_value, preferred_element_type=jnp.float32).astype(jnp.bfloat16)
    position = lax.broadcasted_iota(jnp.int32, (regions, N_TM, TCH), 2)
    valid = position < live_counts[:, :, None]
    query_live = valid.reshape(regions * total_time, 1).astype(jnp.float32)
    grad_proj = (jnp.dot(output_grad.reshape(-1, model_width), w_out.T, preferred_element_type=jnp.float32) * query_live).astype(jnp.bfloat16)

    def by_span(array_in):
        return array_in.reshape(regions, N_TM, TCH, model_width).transpose(1, 0, 2, 3).reshape(N_TM, regions * TCH, model_width)
    key_mask = valid.transpose(1, 0, 2).reshape(N_TM, regions * TCH)
    query_part, side_part = lax.map(make_span_grads(w_key, w_value), (by_span(queries), by_span(key_proj), by_span(value_proj), by_span(grad_proj), key_mask))

    def by_region(array_in):
        return array_in.reshape(N_TM, regions, TCH, model_width).transpose(1, 0, 2, 3).reshape(-1, model_width)
    query_grad = by_region(query_part).astype(jnp.bfloat16)
    side_grad = by_region(side_part)
    hidden_grad = jnp.dot(query_grad, w_query.T, preferred_element_type=jnp.float32) + side_grad
    input_grad = conv_transpose(hidden_grad.reshape(regions, total_time, model_width), conv_kernel)
    return input_grad.astype(jnp.bfloat16)
```

```python
import functools
import math

import jax
import jax.numpy as jnp
from jax import lax
from jax.experimental import pallas as pl
from jax.experimental.pallas import tpu as pltpu
from jax.sharding import PartitionSpec as P

H = 12
KW = 4
BLK = 256
NEG = -1e30
bf16 = jnp.bfloat16
f32 = jnp.float32
VM = pl.BlockSpec(memory_space=pltpu.VMEM)
SM = pl.BlockSpec(memory_space=pltpu.SMEM)
ANY = pl.BlockSpec(memory_space=pl.ANY)
MESH = pl.DeviceIdType.MESH


def dot(a, b):
    return jnp.dot(a, b, preferred_element_type=f32)


def dot_t(a, b):
    return lax.dot_general(a, b, (((1,), (1,)), ((), ())), preferred_element_type=f32)


def owner(h, n_reg):
    return (h * n_reg) // H


def head_of(me, n_reg):
    h = (me * H + n_reg - 1) // n_reg
    return h, jnp.logical_and(h < H, owner(h, n_reg) == me)


def enter(n_reg, n_tm, me, mt):
    barrier = pltpu.get_barrier_semaphore()
    for d in range(1, n_reg):
        pl.semaphore_signal(
            barrier,
            inc=1,
            device_id={"region": lax.rem(me + d, n_reg)},
            device_id_type=MESH,
        )
    if n_tm > 1:

        @pl.when(mt > 0)
        def _():
            pl.semaphore_signal(barrier, inc=1, device_id={"tm": mt - 1}, device_id_type=MESH)

        @pl.when(mt < n_tm - 1)
        def _():
            pl.semaphore_signal(barrier, inc=1, device_id={"tm": mt + 1}, device_id_type=MESH)

    def settle():
        peers = n_reg - 1 + jnp.minimum(mt, 1) + jnp.minimum(n_tm - 1 - mt, 1)
        pl.semaphore_wait(barrier, peers)

    return settle


def spread_kernel(
    n_reg, n_tm, lat_ref, og_ref, ck_ref, cnt_ref, wq_ref, wk_ref, wv_ref, wo_ref,
    out_ref, cout_ref,
    wbuf, ext, edge, send, csend, wsem, esem, ssem, rsem, cssem, crsem, lsem,
):
    me = lax.axis_index("region")
    mt = lax.axis_index("tm")
    t, d = lat_ref.shape[1], lat_ref.shape[2]
    hd = d // H
    loads = [
        pltpu.make_async_copy(ref, wbuf.at[i], wsem.at[i])
        for i, ref in enumerate((wo_ref, wq_ref, wk_ref, wv_ref))
    ]
    for load in loads:
        load.start()
    settle = enter(n_reg, n_tm, me, mt)
    count = cnt_ref[0, 0]
    csend[...] = jnp.zeros(csend.shape, jnp.int32) + count
    settle()
    to_next = pltpu.make_async_remote_copy(
        src_ref=lat_ref.at[0, pl.ds(t - 16, 16)],
        dst_ref=edge,
        send_sem=esem.at[0],
        recv_sem=esem.at[1],
        device_id={"tm": jnp.minimum(mt + 1, n_tm - 1)},
        device_id_type=MESH,
    )

    @pl.when(mt < n_tm - 1)
    def _():
        to_next.start()

    ext[8 : 8 + t, :] = lat_ref[0].astype(f32)
    loads[0].wait()
    live = lax.broadcasted_iota(jnp.int32, (t, 1), 0) < count
    g = dot_t(og_ref[0], wbuf[0])
    g = jnp.where(live, g, 0.0).astype(bf16)
    for h in range(H):
        send[h, :, 3 * hd : 4 * hd] = g[:, h * hd : (h + 1) * hd]

    @pl.when(mt == 0)
    def _():
        ext[0:8, :] = jnp.zeros((8, d), f32)

    @pl.when(mt > 0)
    def _():
        to_next.wait_recv()
        ext[0:8, :] = edge[8:16, :].astype(f32)

    hidden = ck_ref[0:1, :] * ext[8 : 8 + t, :]
    for j in range(1, KW):
        hidden = hidden + ck_ref[j : j + 1, :] * ext[8 - j : 8 - j + t, :]
    hidden = hidden.astype(bf16)
    for i in range(3):
        loads[i + 1].wait()
        x = dot(hidden, wbuf[i + 1]).astype(bf16)
        for h in range(H):
            send[h, :, i * hd : (i + 1) * hd] = x[:, h * hd : (h + 1) * hd]

    def copies(i):
        h = lax.rem(me + i, H)
        target = owner(h, n_reg)
        big = pltpu.make_async_remote_copy(
            src_ref=send.at[h],
            dst_ref=out_ref.at[me],
            send_sem=ssem.at[i],
            recv_sem=rsem.at[me],
            device_id={"region": target},
            device_id_type=MESH,
        )
        small = pltpu.make_async_remote_copy(
            src_ref=csend,
            dst_ref=cout_ref.at[me],
            send_sem=cssem.at[i],
            recv_sem=crsem.at[me],
            device_id={"region": target},
            device_id_type=MESH,
        )
        here = pltpu.make_async_copy(send.at[h], out_ref.at[me], lsem.at[0])
        chere = pltpu.make_async_copy(csend, cout_ref.at[me], lsem.at[1])
        return target, big, small, here, chere

    for i in range(H):
        target, big, small, here, chere = copies(i)

        @pl.when(target != me)
        def _():
            small.start()
            big.start()

        @pl.when(target == me)
        def _():
            chere.start()
            here.start()

    for i in range(H):
        target, big, small, here, chere = copies(i)

        @pl.when(target != me)
        def _():
            small.wait_send()
            big.wait_send()

        @pl.when(target == me)
        def _():
            chere.wait()
            here.wait()

    @pl.when(mt < n_tm - 1)
    def _():
        to_next.wait_send()

    _, is_head = head_of(me, n_reg)

    @pl.when(is_head)
    def _():
        for k in range(1, n_reg):
            s = lax.rem(me + k, n_reg)
            pltpu.make_async_copy(csend, cout_ref.at[s], crsem.at[s]).wait()
            pltpu.make_async_copy(send.at[0], out_ref.at[s], rsem.at[s]).wait()


def attend_kernel(
    n_reg, hd, chunk_ref, cnt_ref, out_ref, qk, ka, vg, kt, sbuf, wbuf, dkv, dqp
):
    me = lax.axis_index("region")
    t = chunk_ref.shape[1]
    inv_root = 1.0 / math.sqrt(hd)
    _, is_head = head_of(me, n_reg)

    def lane(rows):
        return lax.broadcasted_iota(jnp.int32, (rows, 2 * hd), 1)

    @pl.when(is_head)
    def _():
        def put(off, rows, a, b, live):
            low = lane(rows) < hd
            bias = jnp.where(jnp.logical_and(lane(rows) == 0, jnp.logical_not(live)), NEG, 0.0)
            qk[pl.ds(off, rows), :] = a
            ka[pl.ds(off, rows), :] = jnp.where(low, bias, a.astype(f32)).astype(bf16)
            vg[pl.ds(off, rows), :] = b

        def pack(r, off):
            off = pl.multiple_of(off, 16)
            count = cnt_ref[r, 0, 0]
            live = lax.broadcasted_iota(jnp.int32, (t, 2 * hd), 0) < count
            put(off, t, chunk_ref[r, :, 0 : 2 * hd], chunk_ref[r, :, 2 * hd : 4 * hd], live)
            return off + (count + 15) // 16 * 16

        total = pl.multiple_of(lax.fori_loop(0, n_reg, pack, 0), 16)
        blank = jnp.zeros((BLK, 2 * hd), bf16)
        put(total, BLK, blank, blank, jnp.zeros((BLK, 2 * hd), jnp.int32) > 0)
        blocks = (total + BLK - 1) // BLK

        def ready(i, c):
            at = pl.multiple_of(i * BLK, BLK)
            kt[i] = ka[pl.ds(at, BLK), :].T[hd:, :]
            dkv[pl.ds(at, BLK), :] = jnp.zeros((BLK, 2 * hd), f32)
            return c

        lax.fori_loop(0, blocks, ready, 0)

        def per_queries(qi, c):
            at = pl.multiple_of(qi * BLK, BLK)
            a = qk[pl.ds(at, BLK), :]
            b = vg[pl.ds(at, BLK), :]
            scaled = a.astype(f32) * inv_root
            low = lane(BLK) < hd
            one = jnp.where(lax.broadcasted_iota(jnp.int32, (hd, BLK), 0) == 0, 1.0, 0.0)
            q_t = scaled.T[0:hd, :]
            qat = jnp.concatenate([one, q_t], axis=0).astype(bf16)
            g_t = b.astype(f32).T[hd:, :]
            gat = jnp.concatenate([g_t, jnp.zeros((hd, BLK), f32)], axis=0).astype(bf16)
            qg = jnp.concatenate(
                [jnp.where(low, scaled, 0.0), jnp.where(low, 0.0, b.astype(f32))], axis=0
            ).astype(bf16)

            def first(ki, carry):
                m, l, dl = carry
                kat = pl.multiple_of(ki * BLK, BLK)
                s = dot(ka[pl.ds(kat, BLK), :], qat)
                w = dot(vg[pl.ds(kat, BLK), :], gat)
                sbuf[ki] = s
                wbuf[ki] = w
                m2 = jnp.maximum(m, jnp.max(s, axis=0, keepdims=True))
                p = jnp.exp(s - m2)
                r = jnp.exp(m - m2)
                l = l * r + jnp.sum(p, axis=0, keepdims=True)
                dl = dl * r + jnp.sum(p * w, axis=0, keepdims=True)
                return m2, l, dl

            m, l, dl = lax.fori_loop(
                0,
                blocks,
                first,
                (jnp.full((1, BLK), NEG, f32), jnp.zeros((1, BLK), f32), jnp.zeros((1, BLK), f32)),
            )
            log_total = m + jnp.log(l)
            delta = dl / l

            def second(ki, dq):
                kat = pl.multiple_of(ki * BLK, BLK)
                att = jnp.exp(sbuf[ki] - log_total)
                ds = (att * (wbuf[ki] - delta)).astype(bf16)
                dkv[pl.ds(kat, BLK), :] += dot(jnp.concatenate([ds, att.astype(bf16)], axis=1), qg)
                return dq + dot(kt[ki], ds)

            dq = lax.fori_loop(0, blocks, second, jnp.zeros((hd, BLK), f32))
            dq = jnp.concatenate([dq * inv_root, jnp.zeros((hd, BLK), f32)], axis=0)
            dqp[pl.ds(at, BLK), :] = dq.T
            return c

        lax.fori_loop(0, blocks, per_queries, 0)

        def unpack(r, off):
            off = pl.multiple_of(off, 16)
            count = cnt_ref[r, 0, 0]
            live = lax.broadcasted_iota(jnp.int32, (t, 2 * hd), 0) < count
            both = jnp.where(live, dkv[pl.ds(off, t), :], 0.0)
            dq = jnp.where(live, dqp[pl.ds(off, t), :], 0.0)
            out_ref[r, 0:t, :] = both.astype(bf16)
            pair = jnp.concatenate([dq[0 : t // 2, 0:hd], dq[t // 2 :, 0:hd]], axis=1)
            out_ref[r, t:, :] = pair.astype(bf16)
            return off + (count + 15) // 16 * 16

        lax.fori_loop(0, n_reg, unpack, 0)


def collect_kernel(
    n_reg, n_tm, part_ref, ck_ref, wq_ref, wk_ref, wv_ref,
    out_ref,
    got, wbuf, xs, ext, wsem, esem, ssem, rsem, lsem,
):
    me = lax.axis_index("region")
    mt = lax.axis_index("tm")
    t, d = out_ref.shape[1], out_ref.shape[2]
    hd = d // H
    loads = [
        pltpu.make_async_copy(ref, wbuf.at[i], wsem.at[i])
        for i, ref in enumerate((wq_ref, wk_ref, wv_ref))
    ]
    for load in loads:
        load.start()
    settle = enter(n_reg, n_tm, me, mt)
    settle()
    head, is_head = head_of(me, n_reg)
    head = jnp.minimum(head, H - 1)

    def away(k):
        r = lax.rem(me + k, n_reg)
        return pltpu.make_async_remote_copy(
            src_ref=part_ref.at[r],
            dst_ref=got.at[head],
            send_sem=ssem.at[k],
            recv_sem=rsem.at[head],
            device_id={"region": r},
            device_id_type=MESH,
        )

    here = pltpu.make_async_copy(part_ref.at[me], got.at[head], lsem)

    @pl.when(is_head)
    def _():
        for k in range(1, n_reg):
            away(k).start()
        here.start()
        here.wait()

    for h in range(H):

        @pl.when(owner(h, n_reg) != me)
        def _():
            pltpu.make_async_copy(part_ref.at[0], got.at[h], rsem.at[h]).wait()

    for h in range(H):
        cols = slice(h * hd, (h + 1) * hd)
        xs[0, 0 : t // 2, cols] = got[h, t:, 0:hd]
        xs[0, t // 2 :, cols] = got[h, t:, hd:]
        xs[1, :, cols] = got[h, 0:t, 0:hd]
        xs[2, :, cols] = got[h, 0:t, hd:]
    for load in loads:
        load.wait()
    side = dot_t(xs[1], wbuf[1]) + dot_t(xs[2], wbuf[2])
    ext[0:t, :] = dot_t(xs[0], wbuf[0]) + side

    to_prev = pltpu.make_async_remote_copy(
        src_ref=ext.at[pl.ds(0, 8)],
        dst_ref=ext.at[pl.ds(t, 8)],
        send_sem=esem.at[0],
        recv_sem=esem.at[1],
        device_id={"tm": jnp.maximum(mt - 1, 0)},
        device_id_type=MESH,
    )

    @pl.when(mt > 0)
    def _():
        to_prev.start()

    @pl.when(is_head)
    def _():
        for k in range(1, n_reg):
            away(k).wait_send()

    @pl.when(mt == n_tm - 1)
    def _():
        ext[t : t + 8, :] = jnp.zeros((8, d), f32)

    @pl.when(mt < n_tm - 1)
    def _():
        to_prev.wait_recv()

    total = ck_ref[0:1, :] * ext[0:t, :]
    for j in range(1, KW):
        total = total + ck_ref[j : j + 1, :] * ext[j : j + t, :]
    out_ref[0] = total.astype(bf16)

    @pl.when(mt > 0)
    def _():
        to_prev.wait_send()


def shards(n_reg, n_tm, latents, output_grad, conv_kernel, w_query, w_key, w_value, w_out, live_counts):
    _, t, d = latents.shape
    hd = d // H
    dma = pltpu.SemaphoreType.DMA
    n = n_reg * t
    blocks = -(-n // BLK)
    chunks, counts = pl.pallas_call(
        functools.partial(spread_kernel, n_reg, n_tm),
        out_shape=(
            jax.ShapeDtypeStruct((n_reg, t, 4 * hd), bf16),
            jax.ShapeDtypeStruct((n_reg, 1, 128), jnp.int32),
        ),
        in_specs=[VM, VM, VM, SM, ANY, ANY, ANY, ANY],
        out_specs=(ANY, ANY),
        scratch_shapes=[
            pltpu.VMEM((4, d, d), bf16),
            pltpu.VMEM((t + 8, d), f32),
            pltpu.VMEM((16, d), bf16),
            pltpu.VMEM((H, t, 4 * hd), bf16),
            pltpu.VMEM((1, 128), jnp.int32),
            dma((4,)),
            dma((2,)),
            dma((H,)),
            dma((n_reg,)),
            dma((H,)),
            dma((n_reg,)),
            dma((2,)),
        ],
        compiler_params=pltpu.CompilerParams(collective_id=0, has_side_effects=True),
        name="spread",
    )(latents, output_grad, conv_kernel, live_counts, w_query, w_key, w_value, w_out)
    part = pl.pallas_call(
        functools.partial(attend_kernel, n_reg, hd),
        out_shape=jax.ShapeDtypeStruct((n_reg, t + t // 2, 2 * hd), bf16),
        in_specs=[VM, SM],
        out_specs=VM,
        scratch_shapes=[
            pltpu.VMEM((n + BLK, 2 * hd), bf16),
            pltpu.VMEM((n + BLK, 2 * hd), bf16),
            pltpu.VMEM((n + BLK, 2 * hd), bf16),
            pltpu.VMEM((blocks, hd, BLK), bf16),
            pltpu.VMEM((blocks, BLK, BLK), f32),
            pltpu.VMEM((blocks, BLK, BLK), f32),
            pltpu.VMEM((n + BLK, 2 * hd), f32),
            pltpu.VMEM((n + BLK, 2 * hd), f32),
        ],
        name="attend",
    )(chunks, counts)
    return pl.pallas_call(
        functools.partial(collect_kernel, n_reg, n_tm),
        out_shape=jax.ShapeDtypeStruct((1, t, d), bf16),
        in_specs=[ANY, VM, ANY, ANY, ANY],
        out_specs=VM,
        scratch_shapes=[
            pltpu.VMEM((H, t + t // 2, 2 * hd), bf16),
            pltpu.VMEM((3, d, d), bf16),
            pltpu.VMEM((3, t, d), bf16),
            pltpu.VMEM((t + 8, d), f32),
            dma((3,)),
            dma((2,)),
            dma((n_reg,)),
            dma((H,)),
            dma,
        ],
        compiler_params=pltpu.CompilerParams(collective_id=1, has_side_effects=True),
        name="collect",
    )(part, conv_kernel, w_query, w_key, w_value)


def solution(mesh):
    shard = P("region", "tm", None)
    in_specs = (shard, shard, P(), P(), P(), P(), P(), P("region", "tm"))
    body = functools.partial(shards, mesh.shape["region"], mesh.shape["tm"])
    return jax.shard_map(body, mesh=mesh, in_specs=in_specs, out_specs=shard, check_vma=False)
```

```python
import functools
import math

import jax
import jax.numpy as jnp
from jax import lax
from jax.experimental import pallas as pl
from jax.experimental.pallas import tpu as pltpu
from jax.sharding import PartitionSpec as P

H = 12
KW = 4
BLK = 256
KBLK = 1024
NEG = -1e30
bf16 = jnp.bfloat16
f32 = jnp.float32
VM = pl.BlockSpec(memory_space=pltpu.VMEM)
SM = pl.BlockSpec(memory_space=pltpu.SMEM)
ANY = pl.BlockSpec(memory_space=pl.ANY)
MESH = pl.DeviceIdType.MESH


def dot(a, b):
    return jnp.dot(a, b, preferred_element_type=f32)


def dot_t(a, b):
    return lax.dot_general(a, b, (((1,), (1,)), ((), ())), preferred_element_type=f32)


def owner(h, n_reg):
    return (h * n_reg) // H


def head_of(me, n_reg):
    h = (me * H + n_reg - 1) // n_reg
    return h, jnp.logical_and(h < H, owner(h, n_reg) == me)


def enter(n_reg, n_tm, me, mt):
    barrier = pltpu.get_barrier_semaphore()
    for d in range(1, n_reg):
        pl.semaphore_signal(
            barrier,
            inc=1,
            device_id={"region": lax.rem(me + d, n_reg)},
            device_id_type=MESH,
        )
    if n_tm > 1:

        @pl.when(mt > 0)
        def _():
            pl.semaphore_signal(barrier, inc=1, device_id={"tm": mt - 1}, device_id_type=MESH)

        @pl.when(mt < n_tm - 1)
        def _():
            pl.semaphore_signal(barrier, inc=1, device_id={"tm": mt + 1}, device_id_type=MESH)

    def settle():
        peers = n_reg - 1 + jnp.minimum(mt, 1) + jnp.minimum(n_tm - 1 - mt, 1)
        pl.semaphore_wait(barrier, peers)

    return settle


def spread_kernel(
    n_reg, n_tm, lat_ref, og_ref, ck_ref, cnt_ref, wq_ref, wk_ref, wv_ref, wo_ref,
    out_ref, cout_ref,
    wbuf, ext, edge, send, csend, wsem, esem, ssem, rsem, cssem, crsem, lsem,
):
    me = lax.axis_index("region")
    mt = lax.axis_index("tm")
    t, d = lat_ref.shape[1], lat_ref.shape[2]
    hd = d // H
    loads = [
        pltpu.make_async_copy(ref, wbuf.at[i], wsem.at[i])
        for i, ref in enumerate((wo_ref, wq_ref, wk_ref, wv_ref))
    ]
    for load in loads:
        load.start()
    settle = enter(n_reg, n_tm, me, mt)
    count = cnt_ref[0, 0]
    csend[...] = jnp.zeros(csend.shape, jnp.int32) + count
    settle()
    to_next = pltpu.make_async_remote_copy(
        src_ref=lat_ref.at[0, pl.ds(t - 16, 16)],
        dst_ref=edge,
        send_sem=esem.at[0],
        recv_sem=esem.at[1],
        device_id={"tm": jnp.minimum(mt + 1, n_tm - 1)},
        device_id_type=MESH,
    )

    @pl.when(mt < n_tm - 1)
    def _():
        to_next.start()

    ext[8 : 8 + t, :] = lat_ref[0].astype(f32)
    loads[0].wait()
    live = lax.broadcasted_iota(jnp.int32, (t, 1), 0) < count
    g = dot_t(og_ref[0], wbuf[0])
    g = jnp.where(live, g, 0.0).astype(bf16)
    for h in range(H):
        send[h, :, 3 * hd : 4 * hd] = g[:, h * hd : (h + 1) * hd]

    @pl.when(mt == 0)
    def _():
        ext[0:8, :] = jnp.zeros((8, d), f32)

    @pl.when(mt > 0)
    def _():
        to_next.wait_recv()
        ext[0:8, :] = edge[8:16, :].astype(f32)

    hidden = ck_ref[0:1, :] * ext[8 : 8 + t, :]
    for j in range(1, KW):
        hidden = hidden + ck_ref[j : j + 1, :] * ext[8 - j : 8 - j + t, :]
    hidden = hidden.astype(bf16)
    for i in range(3):
        loads[i + 1].wait()
        x = dot(hidden, wbuf[i + 1]).astype(bf16)
        for h in range(H):
            send[h, :, i * hd : (i + 1) * hd] = x[:, h * hd : (h + 1) * hd]

    def copies(i):
        h = lax.rem(me + i, H)
        target = owner(h, n_reg)
        big = pltpu.make_async_remote_copy(
            src_ref=send.at[h],
            dst_ref=out_ref.at[me],
            send_sem=ssem.at[i],
            recv_sem=rsem.at[me],
            device_id={"region": target},
            device_id_type=MESH,
        )
        small = pltpu.make_async_remote_copy(
            src_ref=csend,
            dst_ref=cout_ref.at[me],
            send_sem=cssem.at[i],
            recv_sem=crsem.at[me],
            device_id={"region": target},
            device_id_type=MESH,
        )
        here = pltpu.make_async_copy(send.at[h], out_ref.at[me], lsem.at[0])
        chere = pltpu.make_async_copy(csend, cout_ref.at[me], lsem.at[1])
        return target, big, small, here, chere

    for i in range(H):
        target, big, small, here, chere = copies(i)

        @pl.when(target != me)
        def _():
            small.start()
            big.start()

        @pl.when(target == me)
        def _():
            chere.start()
            here.start()

    for i in range(H):
        target, big, small, here, chere = copies(i)

        @pl.when(target != me)
        def _():
            small.wait_send()
            big.wait_send()

        @pl.when(target == me)
        def _():
            chere.wait()
            here.wait()

    @pl.when(mt < n_tm - 1)
    def _():
        to_next.wait_send()

    _, is_head = head_of(me, n_reg)

    @pl.when(is_head)
    def _():
        for k in range(1, n_reg):
            s = lax.rem(me + k, n_reg)
            pltpu.make_async_copy(csend, cout_ref.at[s], crsem.at[s]).wait()
            pltpu.make_async_copy(send.at[0], out_ref.at[s], rsem.at[s]).wait()


def attend_kernel(
    n_reg, hd, chunk_ref, cnt_ref, out_ref, qk, ka, vg, kt, qt, gt, qg, sbuf, wbuf, dkv, dqp
):
    me = lax.axis_index("region")
    t = chunk_ref.shape[1]
    inv_root = 1.0 / math.sqrt(hd)
    _, is_head = head_of(me, n_reg)
    width = 2 * hd
    subs = KBLK // BLK

    def lane(rows):
        return lax.broadcasted_iota(jnp.int32, (rows, width), 1)

    @pl.when(is_head)
    def _():
        def pack(r, off):
            off = pl.multiple_of(off, 16)
            count = cnt_ref[r, 0, 0]
            a = chunk_ref[r, :, 0:width]
            dead = lax.broadcasted_iota(jnp.int32, (t, width), 0) >= count
            bias = jnp.where(jnp.logical_and(lane(t) == 0, dead), NEG, 0.0)
            qk[pl.ds(off, t), :] = a
            ka[pl.ds(off, t), :] = jnp.where(lane(t) < hd, bias, a.astype(f32)).astype(bf16)
            vg[pl.ds(off, t), :] = chunk_ref[r, :, width : 2 * width]
            return off + (count + 15) // 16 * 16

        total = pl.multiple_of(lax.fori_loop(0, n_reg, pack, 0, unroll=4), 16)
        blank = jnp.zeros((KBLK, width), bf16)
        qk[pl.ds(total, KBLK), :] = blank
        ka[pl.ds(total, KBLK), :] = jnp.where(lane(KBLK) == 0, NEG, 0.0).astype(bf16)
        vg[pl.ds(total, KBLK), :] = blank
        blocks = (total + BLK - 1) // BLK
        supers = (total + KBLK - 1) // KBLK

        def ready(i, c):
            at = pl.multiple_of(i * BLK, BLK)
            a = qk[pl.ds(at, BLK), :]
            b = vg[pl.ds(at, BLK), :]
            a_t = a.T
            scaled = (a_t[0:hd, :].astype(f32) * inv_root).astype(bf16)
            one = jnp.where(lax.broadcasted_iota(jnp.int32, (hd, BLK), 0) == 0, 1.0, 0.0)
            qt[i] = jnp.concatenate([one.astype(bf16), scaled], axis=0)
            kt[i] = a_t[hd:, :]
            gt[i] = jnp.concatenate([b.T[hd:, :], jnp.zeros((hd, BLK), bf16)], axis=0)
            low = lane(BLK) < hd
            qg[i, 0:BLK, :] = jnp.where(low, a.astype(f32) * inv_root, 0.0).astype(bf16)
            qg[i, BLK:, :] = jnp.where(low, 0.0, b.astype(f32)).astype(bf16)
            dkv[pl.ds(at, BLK), :] = jnp.zeros((BLK, width), f32)
            return c

        lax.fori_loop(0, supers * subs, ready, 0)

        def fold(x, op):
            return op(x.reshape(BLK // 8, 8, BLK), axis=0)

        def per_queries(qi, c):
            at = pl.multiple_of(qi * BLK, BLK)
            qat, gat = qt[qi], gt[qi]

            def first(ki, m):
                for u in range(subs):
                    kat = pl.multiple_of(ki * KBLK + u * BLK, BLK)
                    s = dot(ka[pl.ds(kat, BLK), :], qat)
                    wbuf[ki * subs + u] = dot(vg[pl.ds(kat, BLK), :], gat)
                    sbuf[ki * subs + u] = s
                    m = jnp.maximum(m, fold(s, jnp.max))
                return m

            m = lax.fori_loop(0, supers, first, jnp.full((8, BLK), NEG, f32))
            m = jnp.max(m, axis=0, keepdims=True)

            def middle(ki, carry):
                l, dl = carry
                for u in range(subs):
                    p = jnp.exp(sbuf[ki * subs + u] - m)
                    sbuf[ki * subs + u] = p
                    l = l + fold(p, jnp.sum)
                    dl = dl + fold(p * wbuf[ki * subs + u], jnp.sum)
                return l, dl

            none = jnp.zeros((8, BLK), f32)
            l, dl = lax.fori_loop(0, supers, middle, (none, none))
            inv_l = 1.0 / jnp.sum(l, axis=0, keepdims=True)
            delta = jnp.sum(dl, axis=0, keepdims=True) * inv_l
            both = qg[qi]

            def last(ki, dq):
                for u in range(subs):
                    kat = pl.multiple_of(ki * KBLK + u * BLK, BLK)
                    att = sbuf[ki * subs + u] * inv_l
                    ds = (att * (wbuf[ki * subs + u] - delta)).astype(bf16)
                    pair = jnp.concatenate([ds, att.astype(bf16)], axis=1)
                    dkv[pl.ds(kat, BLK), :] += dot(pair, both)
                    dq = dq + dot(kt[ki * subs + u], ds)
                return dq

            dq = lax.fori_loop(0, supers, last, jnp.zeros((hd, BLK), f32))
            dq = jnp.concatenate([dq * inv_root, jnp.zeros((hd, BLK), f32)], axis=0)
            dqp[pl.ds(at, BLK), :] = dq.T
            return c

        lax.fori_loop(0, blocks, per_queries, 0)

        def unpack(r, off):
            off = pl.multiple_of(off, 16)
            count = cnt_ref[r, 0, 0]
            live = lax.broadcasted_iota(jnp.int32, (t, width), 0) < count
            both = jnp.where(live, dkv[pl.ds(off, t), :], 0.0)
            dq = jnp.where(live, dqp[pl.ds(off, t), :], 0.0)
            out_ref[r, 0:t, :] = both.astype(bf16)
            pair = jnp.concatenate([dq[0 : t // 2, 0:hd], dq[t // 2 :, 0:hd]], axis=1)
            out_ref[r, t:, :] = pair.astype(bf16)
            return off + (count + 15) // 16 * 16

        lax.fori_loop(0, n_reg, unpack, 0, unroll=4)


def collect_kernel(
    n_reg, n_tm, part_ref, ck_ref, wq_ref, wk_ref, wv_ref,
    out_ref,
    got, wbuf, xs, ext, wsem, esem, ssem, rsem, lsem,
):
    me = lax.axis_index("region")
    mt = lax.axis_index("tm")
    t, d = out_ref.shape[1], out_ref.shape[2]
    hd = d // H
    loads = [
        pltpu.make_async_copy(ref, wbuf.at[i], wsem.at[i])
        for i, ref in enumerate((wq_ref, wk_ref, wv_ref))
    ]
    for load in loads:
        load.start()
    settle = enter(n_reg, n_tm, me, mt)
    settle()
    head, is_head = head_of(me, n_reg)
    head = jnp.minimum(head, H - 1)

    def away(k):
        r = lax.rem(me + k, n_reg)
        return pltpu.make_async_remote_copy(
            src_ref=part_ref.at[r],
            dst_ref=got.at[head],
            send_sem=ssem.at[k],
            recv_sem=rsem.at[head],
            device_id={"region": r},
            device_id_type=MESH,
        )

    here = pltpu.make_async_copy(part_ref.at[me], got.at[head], lsem)

    @pl.when(is_head)
    def _():
        for k in range(1, n_reg):
            away(k).start()
        here.start()
        here.wait()

    for h in range(H):

        @pl.when(owner(h, n_reg) != me)
        def _():
            pltpu.make_async_copy(part_ref.at[0], got.at[h], rsem.at[h]).wait()

    for h in range(H):
        cols = slice(h * hd, (h + 1) * hd)
        xs[0, 0 : t // 2, cols] = got[h, t:, 0:hd]
        xs[0, t // 2 :, cols] = got[h, t:, hd:]
        xs[1, :, cols] = got[h, 0:t, 0:hd]
        xs[2, :, cols] = got[h, 0:t, hd:]
    for load in loads:
        load.wait()
    side = dot_t(xs[1], wbuf[1]) + dot_t(xs[2], wbuf[2])
    ext[0:t, :] = dot_t(xs[0], wbuf[0]) + side

    to_prev = pltpu.make_async_remote_copy(
        src_ref=ext.at[pl.ds(0, 8)],
        dst_ref=ext.at[pl.ds(t, 8)],
        send_sem=esem.at[0],
        recv_sem=esem.at[1],
        device_id={"tm": jnp.maximum(mt - 1, 0)},
        device_id_type=MESH,
    )

    @pl.when(mt > 0)
    def _():
        to_prev.start()

    @pl.when(is_head)
    def _():
        for k in range(1, n_reg):
            away(k).wait_send()

    @pl.when(mt == n_tm - 1)
    def _():
        ext[t : t + 8, :] = jnp.zeros((8, d), f32)

    @pl.when(mt < n_tm - 1)
    def _():
        to_prev.wait_recv()

    total = ck_ref[0:1, :] * ext[0:t, :]
    for j in range(1, KW):
        total = total + ck_ref[j : j + 1, :] * ext[j : j + t, :]
    out_ref[0] = total.astype(bf16)

    @pl.when(mt > 0)
    def _():
        to_prev.wait_send()


def shards(n_reg, n_tm, latents, output_grad, conv_kernel, w_query, w_key, w_value, w_out, live_counts):
    _, t, d = latents.shape
    hd = d // H
    dma = pltpu.SemaphoreType.DMA
    n = n_reg * t
    blocks = -(-n // KBLK) * (KBLK // BLK)
    chunks, counts = pl.pallas_call(
        functools.partial(spread_kernel, n_reg, n_tm),
        out_shape=(
            jax.ShapeDtypeStruct((n_reg, t, 4 * hd), bf16),
            jax.ShapeDtypeStruct((n_reg, 1, 128), jnp.int32),
        ),
        in_specs=[VM, VM, VM, SM, ANY, ANY, ANY, ANY],
        out_specs=(ANY, ANY),
        scratch_shapes=[
            pltpu.VMEM((4, d, d), bf16),
            pltpu.VMEM((t + 8, d), f32),
            pltpu.VMEM((16, d), bf16),
            pltpu.VMEM((H, t, 4 * hd), bf16),
            pltpu.VMEM((1, 128), jnp.int32),
            dma((4,)),
            dma((2,)),
            dma((H,)),
            dma((n_reg,)),
            dma((H,)),
            dma((n_reg,)),
            dma((2,)),
        ],
        compiler_params=pltpu.CompilerParams(collective_id=0, has_side_effects=True),
        name="spread",
    )(latents, output_grad, conv_kernel, live_counts, w_query, w_key, w_value, w_out)
    part = pl.pallas_call(
        functools.partial(attend_kernel, n_reg, hd),
        out_shape=jax.ShapeDtypeStruct((n_reg, t + t // 2, 2 * hd), bf16),
        in_specs=[VM, SM],
        out_specs=VM,
        scratch_shapes=[
            pltpu.VMEM((n + KBLK, 2 * hd), bf16),
            pltpu.VMEM((n + KBLK, 2 * hd), bf16),
            pltpu.VMEM((n + KBLK, 2 * hd), bf16),
            pltpu.VMEM((blocks, hd, BLK), bf16),
            pltpu.VMEM((blocks, 2 * hd, BLK), bf16),
            pltpu.VMEM((blocks, 2 * hd, BLK), bf16),
            pltpu.VMEM((blocks, 2 * BLK, 2 * hd), bf16),
            pltpu.VMEM((blocks, BLK, BLK), f32),
            pltpu.VMEM((blocks, BLK, BLK), f32),
            pltpu.VMEM((n + KBLK, 2 * hd), f32),
            pltpu.VMEM((n + KBLK, 2 * hd), f32),
        ],
        name="attend",
    )(chunks, counts)
    return pl.pallas_call(
        functools.partial(collect_kernel, n_reg, n_tm),
        out_shape=jax.ShapeDtypeStruct((1, t, d), bf16),
        in_specs=[ANY, VM, ANY, ANY, ANY],
        out_specs=VM,
        scratch_shapes=[
            pltpu.VMEM((H, t + t // 2, 2 * hd), bf16),
            pltpu.VMEM((3, d, d), bf16),
            pltpu.VMEM((3, t, d), bf16),
            pltpu.VMEM((t + 8, d), f32),
            dma((3,)),
            dma((2,)),
            dma((n_reg,)),
            dma((H,)),
            dma,
        ],
        compiler_params=pltpu.CompilerParams(collective_id=1, has_side_effects=True),
        name="collect",
    )(part, conv_kernel, w_query, w_key, w_value)


def solution(mesh):
    shard = P("region", "tm", None)
    in_specs = (shard, shard, P(), P(), P(), P(), P(), P("region", "tm"))
    body = functools.partial(shards, mesh.shape["region"], mesh.shape["tm"])
    return jax.shard_map(body, mesh=mesh, in_specs=in_specs, out_specs=shard, check_vma=False)
```

```python
import functools
import math

import jax
import jax.numpy as jnp
from jax import lax
from jax.experimental import pallas as pl
from jax.experimental.pallas import tpu as pltpu
from jax.sharding import PartitionSpec as P

H = 12
KW = 4
BLK = 256
KBLK = 1024
NEG = -1e30
bf16 = jnp.bfloat16
f32 = jnp.float32
VM = pl.BlockSpec(memory_space=pltpu.VMEM)
SM = pl.BlockSpec(memory_space=pltpu.SMEM)
ANY = pl.BlockSpec(memory_space=pl.ANY)
MESH = pl.DeviceIdType.MESH


def dot(a, b):
    return jnp.dot(a, b, preferred_element_type=f32)


def dot_t(a, b):
    return lax.dot_general(a, b, (((1,), (1,)), ((), ())), preferred_element_type=f32)


def owner(h, n_reg):
    return (h * n_reg) // H


def head_of(me, n_reg):
    h = (me * H + n_reg - 1) // n_reg
    return h, jnp.logical_and(h < H, owner(h, n_reg) == me)


def greet(barrier, **where):
    pl.semaphore_signal(barrier, inc=1, device_id=where, device_id_type=MESH)


def spread_kernel(
    n_reg, n_tm, lat_ref, og_ref, ck_ref, cnt_ref, wq_ref, wk_ref, wv_ref, wo_ref,
    out_ref, cout_ref,
    wbuf, ext, edge, send, csend, wsem, esem, ssem, rsem, lsem,
):
    me = lax.axis_index("region")
    mt = lax.axis_index("tm")
    t, d = lat_ref.shape[1], lat_ref.shape[2]
    hd = d // H
    loads = [
        pltpu.make_async_copy(ref, wbuf.at[i], wsem.at[i])
        for i, ref in enumerate((wo_ref, wq_ref, wk_ref, wv_ref))
    ]
    for load in loads:
        load.start()
    barrier = pltpu.get_barrier_semaphore()
    _, is_head = head_of(me, n_reg)

    @pl.when(is_head)
    def _():
        for k in range(1, n_reg):
            greet(barrier, region=lax.rem(me + k, n_reg))

    @pl.when(mt > 0)
    def _():
        greet(barrier, tm=jnp.maximum(mt - 1, 0))

    count = cnt_ref[0, 0]
    csend[...] = jnp.zeros(csend.shape, jnp.int32) + count
    ext[0:8, :] = jnp.zeros((8, d), f32)
    ext[8 : 8 + t, :] = lat_ref[0].astype(f32)
    loads[0].wait()
    live = lax.broadcasted_iota(jnp.int32, (t, 1), 0) < count
    g = dot_t(og_ref[0], wbuf[0])
    g = jnp.where(live, g, 0.0).astype(bf16)
    for h in range(H):
        send[h, :, 3 * hd : 4 * hd] = g[:, h * hd : (h + 1) * hd]

    def project(rows, first):
        hidden = ck_ref[0:1, :] * ext[8 : 8 + rows, :]
        for j in range(1, KW):
            hidden = hidden + ck_ref[j : j + 1, :] * ext[8 - j : 8 - j + rows, :]
        hidden = hidden.astype(bf16)
        for i in range(3):
            if first:
                loads[i + 1].wait()
            x = dot(hidden, wbuf[i + 1]).astype(bf16)
            for h in range(H):
                send[h, 0:rows, i * hd : (i + 1) * hd] = x[:, h * hd : (h + 1) * hd]

    project(t, True)
    heads = H - jnp.where(is_head, 1, 0)
    pl.semaphore_wait(barrier, heads + jnp.minimum(n_tm - 1 - mt, 1))
    to_next = pltpu.make_async_remote_copy(
        src_ref=lat_ref.at[0, pl.ds(t - 16, 16)],
        dst_ref=edge,
        send_sem=esem.at[0],
        recv_sem=esem.at[1],
        device_id={"tm": jnp.minimum(mt + 1, n_tm - 1)},
        device_id_type=MESH,
    )

    @pl.when(mt < n_tm - 1)
    def _():
        to_next.start()

    parts = (pl.ds(16, t - 16), pl.ds(0, 16))

    def target_of(i):
        h = lax.rem(me + i, H)
        return h, owner(h, n_reg)

    def away(i, part):
        h, target = target_of(i)
        return pltpu.make_async_remote_copy(
            src_ref=send.at[h, parts[part]],
            dst_ref=out_ref.at[me, parts[part]],
            send_sem=ssem.at[part, i],
            recv_sem=rsem.at[part, me],
            device_id={"region": target},
            device_id_type=MESH,
        )

    def tell(i):
        return pltpu.make_async_remote_copy(
            src_ref=csend,
            dst_ref=cout_ref.at[me],
            send_sem=ssem.at[2, i],
            recv_sem=rsem.at[2, me],
            device_id={"region": target_of(i)[1]},
            device_id_type=MESH,
        )

    head = jnp.minimum(head_of(me, n_reg)[0], H - 1)
    here = pltpu.make_async_copy(send.at[head], out_ref.at[me], lsem.at[0])
    tell_here = pltpu.make_async_copy(csend, cout_ref.at[me], lsem.at[1])

    for i in range(H):

        @pl.when(target_of(i)[1] != me)
        def _():
            away(i, 0).start()

    @pl.when(mt > 0)
    def _():
        to_next.wait_recv()
        ext[0:8, :] = edge[8:16, :].astype(f32)
        project(16, False)

    for i in range(H):

        @pl.when(target_of(i)[1] != me)
        def _():
            tell(i).start()
            away(i, 1).start()

    @pl.when(is_head)
    def _():
        tell_here.start()
        here.start()
        tell_here.wait()
        here.wait()

    for i in range(H):

        @pl.when(target_of(i)[1] != me)
        def _():
            away(i, 0).wait_send()
            away(i, 1).wait_send()
            tell(i).wait_send()

    @pl.when(mt < n_tm - 1)
    def _():
        to_next.wait_send()

    @pl.when(is_head)
    def _():
        for k in range(1, n_reg):
            s = lax.rem(me + k, n_reg)
            pltpu.make_async_copy(csend, cout_ref.at[s], rsem.at[2, s]).wait()
            for i, rows in enumerate(parts):
                pltpu.make_async_copy(send.at[0, rows], out_ref.at[s, rows], rsem.at[i, s]).wait()


def attend_kernel(
    n_reg, hd, chunk_ref, cnt_ref, out_ref, qk, ka, vg, kt, qt, gt, qg, sbuf, wbuf, dkv, dqp
):
    me = lax.axis_index("region")
    t = chunk_ref.shape[1]
    inv_root = 1.0 / math.sqrt(hd)
    _, is_head = head_of(me, n_reg)
    width = 2 * hd
    subs = KBLK // BLK

    def lane(rows):
        return lax.broadcasted_iota(jnp.int32, (rows, width), 1)

    @pl.when(is_head)
    def _():
        def pack(r, off):
            off = pl.multiple_of(off, 16)
            count = cnt_ref[r, 0, 0]
            a = chunk_ref[r, :, 0:width]
            dead = lax.broadcasted_iota(jnp.int32, (t, width), 0) >= count
            bias = jnp.where(jnp.logical_and(lane(t) == 0, dead), NEG, 0.0)
            qk[pl.ds(off, t), :] = a
            ka[pl.ds(off, t), :] = jnp.where(lane(t) < hd, bias, a.astype(f32)).astype(bf16)
            vg[pl.ds(off, t), :] = chunk_ref[r, :, width : 2 * width]
            return off + (count + 15) // 16 * 16

        total = pl.multiple_of(lax.fori_loop(0, n_reg, pack, 0, unroll=4), 16)
        blank = jnp.zeros((KBLK, width), bf16)
        qk[pl.ds(total, KBLK), :] = blank
        ka[pl.ds(total, KBLK), :] = jnp.where(lane(KBLK) == 0, NEG, 0.0).astype(bf16)
        vg[pl.ds(total, KBLK), :] = blank
        blocks = (total + BLK - 1) // BLK
        supers = (total + KBLK - 1) // KBLK

        def ready(i, c):
            at = pl.multiple_of(i * BLK, BLK)
            a = qk[pl.ds(at, BLK), :]
            b = vg[pl.ds(at, BLK), :]
            a_t = a.T
            scaled = (a_t[0:hd, :].astype(f32) * inv_root).astype(bf16)
            one = jnp.where(lax.broadcasted_iota(jnp.int32, (hd, BLK), 0) == 0, 1.0, 0.0)
            qt[i] = jnp.concatenate([one.astype(bf16), scaled], axis=0)
            kt[i] = a_t[hd:, :]
            gt[i] = jnp.concatenate([b.T[hd:, :], jnp.zeros((hd, BLK), bf16)], axis=0)
            low = lane(BLK) < hd
            qg[i, 0:BLK, :] = jnp.where(low, a.astype(f32) * inv_root, 0.0).astype(bf16)
            qg[i, BLK:, :] = jnp.where(low, 0.0, b.astype(f32)).astype(bf16)
            dkv[pl.ds(at, BLK), :] = jnp.zeros((BLK, width), f32)
            return c

        lax.fori_loop(0, supers * subs, ready, 0)

        def fold(x, op):
            return op(x.reshape(BLK // 8, 8, BLK), axis=0)

        def per_queries(qi, c):
            at = pl.multiple_of(qi * BLK, BLK)
            qat, gat = qt[qi], gt[qi]

            def first(ki, m):
                for u in range(subs):
                    kat = pl.multiple_of(ki * KBLK + u * BLK, BLK)
                    s = dot(ka[pl.ds(kat, BLK), :], qat)
                    wbuf[ki * subs + u] = dot(vg[pl.ds(kat, BLK), :], gat)
                    sbuf[ki * subs + u] = s
                    m = jnp.maximum(m, fold(s, jnp.max))
                return m

            m = lax.fori_loop(0, supers, first, jnp.full((8, BLK), NEG, f32))
            m = jnp.max(m, axis=0, keepdims=True)

            def middle(ki, carry):
                l, dl = carry
                for u in range(subs):
                    p = jnp.exp(sbuf[ki * subs + u] - m)
                    sbuf[ki * subs + u] = p
                    l = l + fold(p, jnp.sum)
                    dl = dl + fold(p * wbuf[ki * subs + u], jnp.sum)
                return l, dl

            none = jnp.zeros((8, BLK), f32)
            l, dl = lax.fori_loop(0, supers, middle, (none, none))
            inv_l = 1.0 / jnp.sum(l, axis=0, keepdims=True)
            delta = jnp.sum(dl, axis=0, keepdims=True) * inv_l
            both = qg[qi]

            def last(ki, dq):
                for u in range(subs):
                    kat = pl.multiple_of(ki * KBLK + u * BLK, BLK)
                    att = sbuf[ki * subs + u] * inv_l
                    ds = (att * (wbuf[ki * subs + u] - delta)).astype(bf16)
                    pair = jnp.concatenate([ds, att.astype(bf16)], axis=1)
                    dkv[pl.ds(kat, BLK), :] += dot(pair, both)
                    dq = dq + dot(kt[ki * subs + u], ds)
                return dq

            dq = lax.fori_loop(0, supers, last, jnp.zeros((hd, BLK), f32))
            dq = jnp.concatenate([dq * inv_root, jnp.zeros((hd, BLK), f32)], axis=0)
            dqp[pl.ds(at, BLK), :] = dq.T
            return c

        lax.fori_loop(0, blocks, per_queries, 0)

        def unpack(r, off):
            off = pl.multiple_of(off, 16)
            count = cnt_ref[r, 0, 0]
            live = lax.broadcasted_iota(jnp.int32, (t, width), 0) < count
            both = jnp.where(live, dkv[pl.ds(off, t), :], 0.0)
            dq = jnp.where(live, dqp[pl.ds(off, t), :], 0.0)
            out_ref[r, 0:t, :] = both.astype(bf16)
            pair = jnp.concatenate([dq[0 : t // 2, 0:hd], dq[t // 2 :, 0:hd]], axis=1)
            out_ref[r, t:, :] = pair.astype(bf16)
            return off + (count + 15) // 16 * 16

        lax.fori_loop(0, n_reg, unpack, 0, unroll=4)


def collect_kernel(
    n_reg, n_tm, part_ref, ck_ref, wq_ref, wk_ref, wv_ref,
    out_ref,
    got, wbuf, xs, ext, wsem, esem, ssem, rsem, lsem,
):
    me = lax.axis_index("region")
    mt = lax.axis_index("tm")
    t, d = out_ref.shape[1], out_ref.shape[2]
    hd = d // H
    loads = [
        pltpu.make_async_copy(ref, wbuf.at[i], wsem.at[i])
        for i, ref in enumerate((wq_ref, wk_ref, wv_ref))
    ]
    for load in loads:
        load.start()
    barrier = pltpu.get_barrier_semaphore()
    head, is_head = head_of(me, n_reg)
    for i in range(H):
        target = owner(lax.rem(me + i, H), n_reg)

        @pl.when(target != me)
        def _():
            greet(barrier, region=target)

    @pl.when(mt < n_tm - 1)
    def _():
        greet(barrier, tm=jnp.minimum(mt + 1, n_tm - 1))

    peers = jnp.where(is_head, n_reg - 1, 0) + jnp.minimum(mt, 1)

    @pl.when(peers > 0)
    def _():
        pl.semaphore_wait(barrier, peers)

    head = jnp.minimum(head, H - 1)

    def away(k):
        r = lax.rem(me + k, n_reg)
        return pltpu.make_async_remote_copy(
            src_ref=part_ref.at[r],
            dst_ref=got.at[head],
            send_sem=ssem.at[k],
            recv_sem=rsem.at[head],
            device_id={"region": r},
            device_id_type=MESH,
        )

    here = pltpu.make_async_copy(part_ref.at[me], got.at[head], lsem)

    @pl.when(is_head)
    def _():
        for k in range(1, n_reg):
            away(k).start()
        here.start()
        here.wait()

    for h in range(H):

        @pl.when(owner(h, n_reg) != me)
        def _():
            pltpu.make_async_copy(part_ref.at[0], got.at[h], rsem.at[h]).wait()

    for h in range(H):
        cols = slice(h * hd, (h + 1) * hd)
        xs[0, 0 : t // 2, cols] = got[h, t:, 0:hd]
        xs[0, t // 2 :, cols] = got[h, t:, hd:]
        xs[1, :, cols] = got[h, 0:t, 0:hd]
        xs[2, :, cols] = got[h, 0:t, hd:]
    for load in loads:
        load.wait()
    side = dot_t(xs[1], wbuf[1]) + dot_t(xs[2], wbuf[2])
    ext[0:t, :] = dot_t(xs[0], wbuf[0]) + side

    to_prev = pltpu.make_async_remote_copy(
        src_ref=ext.at[pl.ds(0, 8)],
        dst_ref=ext.at[pl.ds(t, 8)],
        send_sem=esem.at[0],
        recv_sem=esem.at[1],
        device_id={"tm": jnp.maximum(mt - 1, 0)},
        device_id_type=MESH,
    )

    @pl.when(mt > 0)
    def _():
        to_prev.start()

    @pl.when(is_head)
    def _():
        for k in range(1, n_reg):
            away(k).wait_send()

    @pl.when(mt == n_tm - 1)
    def _():
        ext[t : t + 8, :] = jnp.zeros((8, d), f32)

    @pl.when(mt < n_tm - 1)
    def _():
        to_prev.wait_recv()

    total = ck_ref[0:1, :] * ext[0:t, :]
    for j in range(1, KW):
        total = total + ck_ref[j : j + 1, :] * ext[j : j + t, :]
    out_ref[0] = total.astype(bf16)

    @pl.when(mt > 0)
    def _():
        to_prev.wait_send()


def shards(n_reg, n_tm, latents, output_grad, conv_kernel, w_query, w_key, w_value, w_out, live_counts):
    _, t, d = latents.shape
    hd = d // H
    dma = pltpu.SemaphoreType.DMA
    n = n_reg * t
    blocks = -(-n // KBLK) * (KBLK // BLK)
    chunks, counts = pl.pallas_call(
        functools.partial(spread_kernel, n_reg, n_tm),
        out_shape=(
            jax.ShapeDtypeStruct((n_reg, t, 4 * hd), bf16),
            jax.ShapeDtypeStruct((n_reg, 1, 128), jnp.int32),
        ),
        in_specs=[VM, VM, VM, SM, ANY, ANY, ANY, ANY],
        out_specs=(ANY, ANY),
        scratch_shapes=[
            pltpu.VMEM((4, d, d), bf16),
            pltpu.VMEM((t + 8, d), f32),
            pltpu.VMEM((16, d), bf16),
            pltpu.VMEM((H, t, 4 * hd), bf16),
            pltpu.VMEM((1, 128), jnp.int32),
            dma((4,)),
            dma((2,)),
            dma((3, H)),
            dma((3, n_reg)),
            dma((2,)),
        ],
        compiler_params=pltpu.CompilerParams(collective_id=0, has_side_effects=True),
        name="spread",
    )(latents, output_grad, conv_kernel, live_counts, w_query, w_key, w_value, w_out)
    part = pl.pallas_call(
        functools.partial(attend_kernel, n_reg, hd),
        out_shape=jax.ShapeDtypeStruct((n_reg, t + t // 2, 2 * hd), bf16),
        in_specs=[VM, SM],
        out_specs=VM,
        scratch_shapes=[
            pltpu.VMEM((n + KBLK, 2 * hd), bf16),
            pltpu.VMEM((n + KBLK, 2 * hd), bf16),
            pltpu.VMEM((n + KBLK, 2 * hd), bf16),
            pltpu.VMEM((blocks, hd, BLK), bf16),
            pltpu.VMEM((blocks, 2 * hd, BLK), bf16),
            pltpu.VMEM((blocks, 2 * hd, BLK), bf16),
            pltpu.VMEM((blocks, 2 * BLK, 2 * hd), bf16),
            pltpu.VMEM((blocks, BLK, BLK), f32),
            pltpu.VMEM((blocks, BLK, BLK), f32),
            pltpu.VMEM((n + KBLK, 2 * hd), f32),
            pltpu.VMEM((n + KBLK, 2 * hd), f32),
        ],
        name="attend",
    )(chunks, counts)
    return pl.pallas_call(
        functools.partial(collect_kernel, n_reg, n_tm),
        out_shape=jax.ShapeDtypeStruct((1, t, d), bf16),
        in_specs=[ANY, VM, ANY, ANY, ANY],
        out_specs=VM,
        scratch_shapes=[
            pltpu.VMEM((H, t + t // 2, 2 * hd), bf16),
            pltpu.VMEM((3, d, d), bf16),
            pltpu.VMEM((3, t, d), bf16),
            pltpu.VMEM((t + 8, d), f32),
            dma((3,)),
            dma((2,)),
            dma((n_reg,)),
            dma((H,)),
            dma,
        ],
        compiler_params=pltpu.CompilerParams(collective_id=1, has_side_effects=True),
        name="collect",
    )(part, conv_kernel, w_query, w_key, w_value)


def solution(mesh):
    shard = P("region", "tm", None)
    in_specs = (shard, shard, P(), P(), P(), P(), P(), P("region", "tm"))
    body = functools.partial(shards, mesh.shape["region"], mesh.shape["tm"])
    return jax.shard_map(body, mesh=mesh, in_specs=in_specs, out_specs=shard, check_vma=False)
```

```python
import functools
import math

import jax
import jax.numpy as jnp
from jax import lax
from jax.experimental import pallas as pl
from jax.experimental.pallas import tpu as pltpu
from jax.sharding import PartitionSpec as P

H = 12
KW = 4
BLK = 256
KBLK = 1024
NEG = -1e30
bf16 = jnp.bfloat16
f32 = jnp.float32
VM = pl.BlockSpec(memory_space=pltpu.VMEM)
SM = pl.BlockSpec(memory_space=pltpu.SMEM)
ANY = pl.BlockSpec(memory_space=pl.ANY)
MESH = pl.DeviceIdType.MESH


def dot(a, b):
    return jnp.dot(a, b, preferred_element_type=f32)


def dot_t(a, b):
    return lax.dot_general(a, b, (((1,), (1,)), ((), ())), preferred_element_type=f32)


def owner(h, n_reg):
    return (h * n_reg) // H


def head_of(me, n_reg):
    h = (me * H + n_reg - 1) // n_reg
    return h, jnp.logical_and(h < H, owner(h, n_reg) == me)


def far_first(n):
    return sorted(range(n), key=lambda k: (abs(k - n // 2), k))


def greet(barrier, **where):
    pl.semaphore_signal(barrier, inc=1, device_id=where, device_id_type=MESH)


def spread_kernel(
    n_reg, n_tm, lat_ref, og_ref, ck_ref, cnt_ref, wq_ref, wk_ref, wv_ref, wo_ref,
    out_ref, cout_ref,
    wbuf, ext, edge, send, csend, wsem, esem, ssem, rsem, lsem,
):
    me = lax.axis_index("region")
    mt = lax.axis_index("tm")
    t, d = lat_ref.shape[1], lat_ref.shape[2]
    hd = d // H
    loads = [
        pltpu.make_async_copy(ref, wbuf.at[i], wsem.at[i])
        for i, ref in enumerate((wo_ref, wq_ref, wk_ref, wv_ref))
    ]
    for load in loads:
        load.start()
    barrier = pltpu.get_barrier_semaphore()
    _, is_head = head_of(me, n_reg)

    @pl.when(is_head)
    def _():
        for k in range(1, n_reg):
            greet(barrier, region=lax.rem(me + k, n_reg))

    @pl.when(mt > 0)
    def _():
        greet(barrier, tm=jnp.maximum(mt - 1, 0))

    count = cnt_ref[0, 0]
    csend[...] = jnp.zeros(csend.shape, jnp.int32) + count
    ext[0:8, :] = jnp.zeros((8, d), f32)
    ext[8 : 8 + t, :] = lat_ref[0].astype(f32)
    loads[0].wait()
    live = lax.broadcasted_iota(jnp.int32, (t, 1), 0) < count
    g = dot_t(og_ref[0], wbuf[0])
    g = jnp.where(live, g, 0.0).astype(bf16)
    for h in range(H):
        send[h, :, 3 * hd : 4 * hd] = g[:, h * hd : (h + 1) * hd]

    def project(rows, first):
        hidden = ck_ref[0:1, :] * ext[8 : 8 + rows, :]
        for j in range(1, KW):
            hidden = hidden + ck_ref[j : j + 1, :] * ext[8 - j : 8 - j + rows, :]
        hidden = hidden.astype(bf16)
        for i in range(3):
            if first:
                loads[i + 1].wait()
            x = dot(hidden, wbuf[i + 1]).astype(bf16)
            for h in range(H):
                send[h, 0:rows, i * hd : (i + 1) * hd] = x[:, h * hd : (h + 1) * hd]

    project(t, True)
    heads = H - jnp.where(is_head, 1, 0)
    pl.semaphore_wait(barrier, heads + jnp.minimum(n_tm - 1 - mt, 1))
    to_next = pltpu.make_async_remote_copy(
        src_ref=lat_ref.at[0, pl.ds(t - 16, 16)],
        dst_ref=edge,
        send_sem=esem.at[0],
        recv_sem=esem.at[1],
        device_id={"tm": jnp.minimum(mt + 1, n_tm - 1)},
        device_id_type=MESH,
    )

    @pl.when(mt < n_tm - 1)
    def _():
        to_next.start()

    parts = (pl.ds(16, t - 16), pl.ds(0, 16))

    def target_of(i):
        h = lax.rem(me * H // n_reg + far_first(H)[i], H)
        return h, owner(h, n_reg)

    def away(i, part):
        h, target = target_of(i)
        return pltpu.make_async_remote_copy(
            src_ref=send.at[h, parts[part]],
            dst_ref=out_ref.at[me, parts[part]],
            send_sem=ssem.at[part, i],
            recv_sem=rsem.at[part, me],
            device_id={"region": target},
            device_id_type=MESH,
        )

    def tell(i):
        return pltpu.make_async_remote_copy(
            src_ref=csend,
            dst_ref=cout_ref.at[me],
            send_sem=ssem.at[2, i],
            recv_sem=rsem.at[2, me],
            device_id={"region": target_of(i)[1]},
            device_id_type=MESH,
        )

    head = jnp.minimum(head_of(me, n_reg)[0], H - 1)
    here = pltpu.make_async_copy(send.at[head], out_ref.at[me], lsem.at[0])
    tell_here = pltpu.make_async_copy(csend, cout_ref.at[me], lsem.at[1])

    for i in range(H):

        @pl.when(target_of(i)[1] != me)
        def _():
            away(i, 0).start()

    @pl.when(mt > 0)
    def _():
        to_next.wait_recv()
        ext[0:8, :] = edge[8:16, :].astype(f32)
        project(16, False)

    for i in range(H):

        @pl.when(target_of(i)[1] != me)
        def _():
            tell(i).start()
            away(i, 1).start()

    @pl.when(is_head)
    def _():
        tell_here.start()
        here.start()
        tell_here.wait()
        here.wait()

    for i in range(H):

        @pl.when(target_of(i)[1] != me)
        def _():
            away(i, 0).wait_send()
            away(i, 1).wait_send()
            tell(i).wait_send()

    @pl.when(mt < n_tm - 1)
    def _():
        to_next.wait_send()

    @pl.when(is_head)
    def _():
        for k in range(1, n_reg):
            s = lax.rem(me + k, n_reg)
            pltpu.make_async_copy(csend, cout_ref.at[s], rsem.at[2, s]).wait()
            for i, rows in enumerate(parts):
                pltpu.make_async_copy(send.at[0, rows], out_ref.at[s, rows], rsem.at[i, s]).wait()


def attend_kernel(
    n_reg, hd, chunk_ref, cnt_ref, out_ref, qk, ka, vg, kt, qt, gt, qg, sbuf, wbuf, dkv, dqp
):
    me = lax.axis_index("region")
    t = chunk_ref.shape[1]
    inv_root = 1.0 / math.sqrt(hd)
    _, is_head = head_of(me, n_reg)
    width = 2 * hd
    subs = KBLK // BLK

    def lane(rows):
        return lax.broadcasted_iota(jnp.int32, (rows, width), 1)

    @pl.when(is_head)
    def _():
        def pack(r, off):
            off = pl.multiple_of(off, 16)
            count = cnt_ref[r, 0, 0]
            a = chunk_ref[r, :, 0:width]
            dead = lax.broadcasted_iota(jnp.int32, (t, width), 0) >= count
            bias = jnp.where(jnp.logical_and(lane(t) == 0, dead), NEG, 0.0)
            qk[pl.ds(off, t), :] = a
            ka[pl.ds(off, t), :] = jnp.where(lane(t) < hd, bias, a.astype(f32)).astype(bf16)
            vg[pl.ds(off, t), :] = chunk_ref[r, :, width : 2 * width]
            return off + (count + 15) // 16 * 16

        total = pl.multiple_of(lax.fori_loop(0, n_reg, pack, 0, unroll=4), 16)
        blank = jnp.zeros((KBLK, width), bf16)
        qk[pl.ds(total, KBLK), :] = blank
        ka[pl.ds(total, KBLK), :] = jnp.where(lane(KBLK) == 0, NEG, 0.0).astype(bf16)
        vg[pl.ds(total, KBLK), :] = blank
        blocks = (total + BLK - 1) // BLK
        supers = (total + KBLK - 1) // KBLK

        def ready(i, c):
            at = pl.multiple_of(i * BLK, BLK)
            a = qk[pl.ds(at, BLK), :]
            b = vg[pl.ds(at, BLK), :]
            a_t = a.T
            scaled = (a_t[0:hd, :].astype(f32) * inv_root).astype(bf16)
            one = jnp.where(lax.broadcasted_iota(jnp.int32, (hd, BLK), 0) == 0, 1.0, 0.0)
            qt[i] = jnp.concatenate([one.astype(bf16), scaled], axis=0)
            kt[i] = a_t[hd:, :]
            gt[i] = jnp.concatenate([b.T[hd:, :], jnp.zeros((hd, BLK), bf16)], axis=0)
            low = lane(BLK) < hd
            qg[i, 0:BLK, :] = jnp.where(low, a.astype(f32) * inv_root, 0.0).astype(bf16)
            qg[i, BLK:, :] = jnp.where(low, 0.0, b.astype(f32)).astype(bf16)
            dkv[pl.ds(at, BLK), :] = jnp.zeros((BLK, width), f32)
            return c

        lax.fori_loop(0, supers * subs, ready, 0)

        def fold(x, op):
            return op(x.reshape(BLK // 8, 8, BLK), axis=0)

        def per_queries(qi, c):
            at = pl.multiple_of(qi * BLK, BLK)
            qat, gat = qt[qi], gt[qi]

            def first(ki, m):
                for u in range(subs):
                    kat = pl.multiple_of(ki * KBLK + u * BLK, BLK)
                    s = dot(ka[pl.ds(kat, BLK), :], qat)
                    wbuf[ki * subs + u] = dot(vg[pl.ds(kat, BLK), :], gat)
                    sbuf[ki * subs + u] = s
                    m = jnp.maximum(m, fold(s, jnp.max))
                return m

            m = lax.fori_loop(0, supers, first, jnp.full((8, BLK), NEG, f32))
            m = jnp.max(m, axis=0, keepdims=True)

            def middle(ki, carry):
                l, dl = carry
                for u in range(subs):
                    p = jnp.exp(sbuf[ki * subs + u] - m)
                    sbuf[ki * subs + u] = p
                    l = l + fold(p, jnp.sum)
                    dl = dl + fold(p * wbuf[ki * subs + u], jnp.sum)
                return l, dl

            none = jnp.zeros((8, BLK), f32)
            l, dl = lax.fori_loop(0, supers, middle, (none, none))
            inv_l = 1.0 / jnp.sum(l, axis=0, keepdims=True)
            delta = jnp.sum(dl, axis=0, keepdims=True) * inv_l
            both = qg[qi]

            def last(ki, dq):
                for u in range(subs):
                    kat = pl.multiple_of(ki * KBLK + u * BLK, BLK)
                    att = sbuf[ki * subs + u] * inv_l
                    ds = (att * (wbuf[ki * subs + u] - delta)).astype(bf16)
                    pair = jnp.concatenate([ds, att.astype(bf16)], axis=1)
                    dkv[pl.ds(kat, BLK), :] += dot(pair, both)
                    dq = dq + dot(kt[ki * subs + u], ds)
                return dq

            dq = lax.fori_loop(0, supers, last, jnp.zeros((hd, BLK), f32))
            dq = jnp.concatenate([dq * inv_root, jnp.zeros((hd, BLK), f32)], axis=0)
            dqp[pl.ds(at, BLK), :] = dq.T
            return c

        lax.fori_loop(0, blocks, per_queries, 0)

        def unpack(r, off):
            off = pl.multiple_of(off, 16)
            count = cnt_ref[r, 0, 0]
            live = lax.broadcasted_iota(jnp.int32, (t, width), 0) < count
            both = jnp.where(live, dkv[pl.ds(off, t), :], 0.0)
            dq = jnp.where(live, dqp[pl.ds(off, t), :], 0.0)
            out_ref[r, 0:t, :] = both.astype(bf16)
            pair = jnp.concatenate([dq[0 : t // 2, 0:hd], dq[t // 2 :, 0:hd]], axis=1)
            out_ref[r, t:, :] = pair.astype(bf16)
            return off + (count + 15) // 16 * 16

        lax.fori_loop(0, n_reg, unpack, 0, unroll=4)


def collect_kernel(
    n_reg, n_tm, part_ref, ck_ref, wq_ref, wk_ref, wv_ref,
    out_ref,
    got, wbuf, xs, ext, wsem, esem, ssem, rsem, lsem,
):
    me = lax.axis_index("region")
    mt = lax.axis_index("tm")
    t, d = out_ref.shape[1], out_ref.shape[2]
    hd = d // H
    loads = [
        pltpu.make_async_copy(ref, wbuf.at[i], wsem.at[i])
        for i, ref in enumerate((wq_ref, wk_ref, wv_ref))
    ]
    for load in loads:
        load.start()
    barrier = pltpu.get_barrier_semaphore()
    head, is_head = head_of(me, n_reg)
    for i in range(H):
        target = owner(lax.rem(me + i, H), n_reg)

        @pl.when(target != me)
        def _():
            greet(barrier, region=target)

    @pl.when(mt < n_tm - 1)
    def _():
        greet(barrier, tm=jnp.minimum(mt + 1, n_tm - 1))

    peers = jnp.where(is_head, n_reg - 1, 0) + jnp.minimum(mt, 1)

    @pl.when(peers > 0)
    def _():
        pl.semaphore_wait(barrier, peers)

    head = jnp.minimum(head, H - 1)

    def away(k):
        r = lax.rem(me + k, n_reg)
        return pltpu.make_async_remote_copy(
            src_ref=part_ref.at[r],
            dst_ref=got.at[head],
            send_sem=ssem.at[k],
            recv_sem=rsem.at[head],
            device_id={"region": r},
            device_id_type=MESH,
        )

    here = pltpu.make_async_copy(part_ref.at[me], got.at[head], lsem)

    @pl.when(is_head)
    def _():
        for k in far_first(n_reg):
            if k:
                away(k).start()
        here.start()
        here.wait()

    for h in range(H):

        @pl.when(owner(h, n_reg) != me)
        def _():
            pltpu.make_async_copy(part_ref.at[0], got.at[h], rsem.at[h]).wait()

    for h in range(H):
        cols = slice(h * hd, (h + 1) * hd)
        xs[0, 0 : t // 2, cols] = got[h, t:, 0:hd]
        xs[0, t // 2 :, cols] = got[h, t:, hd:]
        xs[1, :, cols] = got[h, 0:t, 0:hd]
        xs[2, :, cols] = got[h, 0:t, hd:]
    for load in loads:
        load.wait()
    side = dot_t(xs[1], wbuf[1]) + dot_t(xs[2], wbuf[2])
    ext[0:t, :] = dot_t(xs[0], wbuf[0]) + side

    to_prev = pltpu.make_async_remote_copy(
        src_ref=ext.at[pl.ds(0, 8)],
        dst_ref=ext.at[pl.ds(t, 8)],
        send_sem=esem.at[0],
        recv_sem=esem.at[1],
        device_id={"tm": jnp.maximum(mt - 1, 0)},
        device_id_type=MESH,
    )

    @pl.when(mt > 0)
    def _():
        to_prev.start()

    @pl.when(is_head)
    def _():
        for k in range(1, n_reg):
            away(k).wait_send()

    @pl.when(mt == n_tm - 1)
    def _():
        ext[t : t + 8, :] = jnp.zeros((8, d), f32)

    @pl.when(mt < n_tm - 1)
    def _():
        to_prev.wait_recv()

    total = ck_ref[0:1, :] * ext[0:t, :]
    for j in range(1, KW):
        total = total + ck_ref[j : j + 1, :] * ext[j : j + t, :]
    out_ref[0] = total.astype(bf16)

    @pl.when(mt > 0)
    def _():
        to_prev.wait_send()


def shards(n_reg, n_tm, latents, output_grad, conv_kernel, w_query, w_key, w_value, w_out, live_counts):
    _, t, d = latents.shape
    hd = d // H
    dma = pltpu.SemaphoreType.DMA
    n = n_reg * t
    blocks = -(-n // KBLK) * (KBLK // BLK)
    chunks, counts = pl.pallas_call(
        functools.partial(spread_kernel, n_reg, n_tm),
        out_shape=(
            jax.ShapeDtypeStruct((n_reg, t, 4 * hd), bf16),
            jax.ShapeDtypeStruct((n_reg, 1, 128), jnp.int32),
        ),
        in_specs=[VM, VM, VM, SM, ANY, ANY, ANY, ANY],
        out_specs=(ANY, ANY),
        scratch_shapes=[
            pltpu.VMEM((4, d, d), bf16),
            pltpu.VMEM((t + 8, d), f32),
            pltpu.VMEM((16, d), bf16),
            pltpu.VMEM((H, t, 4 * hd), bf16),
            pltpu.VMEM((1, 128), jnp.int32),
            dma((4,)),
            dma((2,)),
            dma((3, H)),
            dma((3, n_reg)),
            dma((2,)),
        ],
        compiler_params=pltpu.CompilerParams(collective_id=0, has_side_effects=True),
        name="spread",
    )(latents, output_grad, conv_kernel, live_counts, w_query, w_key, w_value, w_out)
    part = pl.pallas_call(
        functools.partial(attend_kernel, n_reg, hd),
        out_shape=jax.ShapeDtypeStruct((n_reg, t + t // 2, 2 * hd), bf16),
        in_specs=[VM, SM],
        out_specs=VM,
        scratch_shapes=[
            pltpu.VMEM((n + KBLK, 2 * hd), bf16),
            pltpu.VMEM((n + KBLK, 2 * hd), bf16),
            pltpu.VMEM((n + KBLK, 2 * hd), bf16),
            pltpu.VMEM((blocks, hd, BLK), bf16),
            pltpu.VMEM((blocks, 2 * hd, BLK), bf16),
            pltpu.VMEM((blocks, 2 * hd, BLK), bf16),
            pltpu.VMEM((blocks, 2 * BLK, 2 * hd), bf16),
            pltpu.VMEM((blocks, BLK, BLK), f32),
            pltpu.VMEM((blocks, BLK, BLK), f32),
            pltpu.VMEM((n + KBLK, 2 * hd), f32),
            pltpu.VMEM((n + KBLK, 2 * hd), f32),
        ],
        name="attend",
    )(chunks, counts)
    return pl.pallas_call(
        functools.partial(collect_kernel, n_reg, n_tm),
        out_shape=jax.ShapeDtypeStruct((1, t, d), bf16),
        in_specs=[ANY, VM, ANY, ANY, ANY],
        out_specs=VM,
        scratch_shapes=[
            pltpu.VMEM((H, t + t // 2, 2 * hd), bf16),
            pltpu.VMEM((3, d, d), bf16),
            pltpu.VMEM((3, t, d), bf16),
            pltpu.VMEM((t + 8, d), f32),
            dma((3,)),
            dma((2,)),
            dma((n_reg,)),
            dma((H,)),
            dma,
        ],
        compiler_params=pltpu.CompilerParams(collective_id=1, has_side_effects=True),
        name="collect",
    )(part, conv_kernel, w_query, w_key, w_value)


def solution(mesh):
    shard = P("region", "tm", None)
    in_specs = (shard, shard, P(), P(), P(), P(), P(), P("region", "tm"))
    body = functools.partial(shards, mesh.shape["region"], mesh.shape["tm"])
    return jax.shard_map(body, mesh=mesh, in_specs=in_specs, out_specs=shard, check_vma=False)
```
